256 devices in a mesh: pipe: 16 (over x, z_lo, core), tensor: 16 (over y, z_hi).
Axes of the slice: x: 4, y: 4, z: 8 (z_hi: 4, z_lo: 2; z = z_hi * 2 + z_lo), core: 2. Of those that a mesh axis runs over, the one named last changes fastest.
Arguments:
- hidden: bfloat16 [384, 8192], P('pipe', 'tensor'), may hold values from -64 to 64
- weight: bfloat16 [8192, 131072], P(None, ('pipe', 'tensor')), may hold values from -0.23201941 to 0.23201941
- targets: int32 [384], replicated, may hold values from 0 to 131071
- token_weight: float32 [384], replicated, may hold values from 0.1 to 1
Outputs:
- token_loss: float32 [384], P('pipe')
- hidden_grad: float32 [384, 8192], P('pipe', 'tensor')
The draws below stay inside these ranges and needn't reach their ends.
All inputs are finite; a program needn't handle non-finite values.
Results may differ from the reference program's by a relative error of at most 0.0029.
Values may be sent and summed in bfloat16 or wider, within the bound.
No kernel may reach another device: no remote copies, remote signals or barrier semaphores. Data moves between devices by JAX's collectives and lax.ppermute only.
A program may use at most 128 MiB of HBM per device.

```python
import math
import jax
import jax.numpy as jnp

D = 8192
TOKENS = 384
VOCAB = 131072


scale_base = 3.0


def weight_table(key):
    key_entries = jax.random.fold_in(key, 11)
    key_columns = jax.random.fold_in(key, 12)
    entries = jnp.clip(jax.random.normal(key_entries, (D, VOCAB), jnp.float32), -5.0, 5.0)
    ramp = 0.87 + 0.26 * jnp.arange(VOCAB, dtype=jnp.float32) / VOCAB
    jitter = jax.random.uniform(key_columns, (VOCAB,), jnp.float32, 0.8, 1.2)
    column_scale = ramp * jitter * scale_base / math.sqrt(D)
    return (entries * column_scale[None, :]).astype(jnp.bfloat16)


def draw_weight(key, part):
    return weight_table(key)


def draw_hidden(key, part):
    key_rows = jax.random.fold_in(key, 21)
    base = jnp.clip(jax.random.normal(key_rows, (TOKENS, D), jnp.float32), -6.0, 6.0)
    return base.astype(jnp.bfloat16)


def set_ends(values, key, low, high):
    longest = values.shape.index(max(values.shape))
    spots = []
    for shift in (0, 1):
        where = [jax.random.randint(jax.random.fold_in(key, axis), (), 0, length) for axis, length in enumerate(values.shape)]
        where[longest] = (where[longest] + shift) % values.shape[longest]
        spots.append(tuple(where))
    return values.at[spots[0]].set(low).at[spots[1]].set(high)


def setup_inputs(seed: int = 0) -> dict:
    splits = jax.random.split(jax.random.key(seed), 5)
    hidden = draw_hidden(jax.random.fold_in(splits[4], 71), 0)
    weight = draw_weight(jax.random.fold_in(splits[4], 71), 0)
    targets = set_ends(jax.random.randint(splits[2], (TOKENS,), 0, VOCAB), jax.random.fold_in(splits[2], 1), 0, VOCAB - 1).astype(jnp.int32)
    token_weight = jnp.clip(jnp.exp(jax.random.uniform(splits[3], (TOKENS,), jnp.float32, math.log(0.1), math.log(1.0))), 0.1, 1.0)
    return dict(hidden=hidden, weight=weight, targets=targets, token_weight=token_weight)


loss_scale = 32.0


def reference(hidden, weight, targets, token_weight):
    logits = jnp.dot(hidden, weight, preferred_element_type=jnp.float32)
    global_peak = jnp.max(logits, axis=1)
    global_total = jnp.sum(jnp.exp(logits - global_peak[:, None]), axis=1)
    log_total = global_peak + jnp.log(global_total)
    columns = jnp.arange(VOCAB, dtype=jnp.int32)
    target_hit = targets[:, None] == columns[None, :]
    target_logit = jnp.sum(jnp.where(target_hit, logits, jnp.float32(0.0)), axis=1)
    token_loss = log_total - target_logit
    softmax = jnp.exp(logits - log_total[:, None])
    onehot = target_hit.astype(jnp.float32)
    dlogits = (loss_scale * token_weight[:, None] * (softmax - onehot)).astype(jnp.bfloat16)
    hidden_grad = jnp.dot(dlogits, weight.T, preferred_element_type=jnp.float32)
    return token_loss, hidden_grad
```

```python
import jax
import jax.numpy as jnp
from jax import lax
from jax.experimental import pallas as pl
from jax.experimental.pallas import tpu as pltpu
from jax.sharding import Mesh
from jax.sharding import PartitionSpec as P

AXES = ("px", "pz", "pc", "ty", "tz")
PIPE = ("px", "pz", "pc")
TENSOR = ("ty", "tz")

loss_scale = 32.0
f32 = jnp.float32
bf16 = jnp.bfloat16


def shifted(block, axis, step):
    count = lax.axis_size(axis)
    return lax.ppermute(block, axis, [(i, (i + step) % count) for i in range(count)])


def along_z(block, flip, step):
    pairs = [
        (p * 4 + t, (p ^ flip) * 4 + (t + step) % 4) for p in range(2) for t in range(4)
    ]
    return lax.ppermute(block, ("pz", "tz"), pairs)


def gathered_direct(block, axis):
    return jnp.stack([block] + [shifted(block, axis, -k) for k in (1, 2, 3)])


def gathered_ring(block, axis):
    half = block.shape[0] // 2
    before = shifted(block, axis, 1)
    after = shifted(block, axis, -1)
    far_first = shifted(before[:half], axis, 1)
    far_second = shifted(after[half:], axis, -1)
    return [block, after, before, far_first, far_second]


def reduced_ring(own, axis):
    half = own(2).shape[0] // 2
    near_after, near_before, far = own(1), own(3), own(2).astype(bf16)
    far_first = shifted(far[:half], axis, 1)
    far_second = shifted(far[half:], axis, -1)
    from_before_second = shifted(near_after[half:].astype(bf16), axis, 1)
    from_after_first = shifted(near_before[:half].astype(bf16), axis, -1)
    from_before_first = shifted(
        (near_after[:half] + far_first.astype(f32)).astype(bf16), axis, 1
    )
    from_after_second = shifted(
        (near_before[half:] + far_second.astype(f32)).astype(bf16), axis, -1
    )
    mine = own(0)
    first = mine[:half] + from_after_first.astype(f32) + from_before_first.astype(f32)
    second = mine[half:] + from_before_second.astype(f32) + from_after_second.astype(f32)
    return first, second


def reduced_direct(halves, axis):
    first, second = halves
    blocks = [first[0], first[1], second[0], second[1]]
    total = blocks[0]
    for k in (1, 2, 3):
        total = total + shifted(blocks[k], axis, k)
    return total


def piece(refs, k, j, half):
    if k == 2:
        return refs[3][j, 0] if j < half else refs[4][j - half, 0]
    return refs[{0: 0, 1: 1, 3: 2}[k]][j, 0]


def row_of(place, core, dx, dz, rows):
    px = (place[0] + dx) % 4
    pz = (place[1] + dz) % 2
    pc = (place[2] + core) % 2
    return pl.multiple_of((px * 4 + pz * 2 + pc) * rows, 8)


def logits_kernel(place, *refs):
    a_refs = (refs[0:5], refs[10:15])
    b_refs = (refs[5:10], refs[15:20])
    w_ref, out_ref, acc_ref = refs[20], refs[21], refs[22]
    step = pl.program_id(0)
    rows = out_ref.shape[0] // 16
    total = None
    for dy in range(4):
        lhs_a = [piece(a_refs[c], dx, dy, 2) for c in range(2) for dx in range(4)]
        lhs_b = [piece(b_refs[c], dy, dx, 2) for c in range(2) for dx in range(4)]
        lhs = jnp.concatenate(
            [jnp.concatenate(lhs_a, axis=0), jnp.concatenate(lhs_b, axis=0)], axis=1
        )
        part = jnp.dot(lhs, w_ref[(place[3] + dy) % 4, 0], preferred_element_type=f32)
        total = part if total is None else total + part

    @pl.when(step == 0)
    def _():
        acc_ref[...] = total

    @pl.when(step > 0)
    def _():
        acc_ref[...] += total

    @pl.when(step == 3)
    def _():
        for c in range(2):
            for dx in range(4):
                for dz in range(2):
                    at = ((c * 4 + dx) * 2 + dz) * rows
                    out_ref[pl.ds(row_of(place, c, dx, dz, rows), rows), :] = acc_ref[
                        at : at + rows, :
                    ]


def weight_spec(width, cols):
    return pl.BlockSpec(
        (4, 1, width, cols), lambda i, place: (0, (place[4] + i) % 4, 0, 0)
    )


def logits_of(place, pieces, blocks):
    rows = pieces[0].shape[2] * 8
    specs = [
        pl.BlockSpec((p.shape[0], 1, *p.shape[2:]), lambda i, place: (0, i, 0, 0)) for p in pieces
    ]
    cols = blocks.shape[3]
    return pl.pallas_call(
        logits_kernel,
        out_shape=jax.ShapeDtypeStruct((rows, cols), f32),
        grid_spec=pltpu.PrefetchScalarGridSpec(
            num_scalar_prefetch=1,
            grid=(4,),
            in_specs=[*specs, weight_spec(blocks.shape[2], cols)],
            out_specs=pl.BlockSpec((rows, cols), lambda i, place: (0, 0)),
            scratch_shapes=[pltpu.VMEM((rows, cols), f32)],
        ),
        compiler_params=pltpu.CompilerParams(dimension_semantics=("arbitrary",)),
        name="logits",
    )(place, *pieces, blocks)


def grad_kernel(
    place, logits_ref, log_total_ref, targets_ref, scale_ref, w_ref, keep_a, keep_b, send_a, send_b, dl_ref
):
    rows, cols = logits_ref.shape[0] // 16, logits_ref.shape[1]

    @pl.when(pl.program_id(0) == 0)
    def _():
        columns = place[5] + lax.broadcasted_iota(jnp.int32, (rows, cols), 1)
        for c in range(2):
            for dx in range(4):
                for dz in range(2):
                    here = pl.ds(row_of(place, c, dx, dz, rows), rows)
                    softmax = jnp.exp(logits_ref[here, :] - log_total_ref[here, :])
                    hit = jnp.where(targets_ref[here, :] == columns, 1.0, 0.0)
                    at = ((c * 4 + dx) * 2 + dz) * rows
                    dl_ref[at : at + rows, :] = scale_ref[here, :] * (softmax - hit)

    dlogits = dl_ref[...].astype(bf16)
    half = w_ref.shape[2] // 2
    for dy in range(4):
        part = lax.dot_general(
            dlogits,
            w_ref[(place[3] + dy) % 4, 0],
            (((1,), (1,)), ((), ())),
            preferred_element_type=f32,
        )
        for dx in range(4):
            at = dx * 2 * rows
            keep_a[dx, dy, 0] = part[at : at + 2 * rows, :half]
            keep_b[dy, dx, 0] = part[at : at + 2 * rows, half:]
            at += 8 * rows
            send_a[dx, dy, 0] = part[at : at + 2 * rows, :half].astype(bf16)
            send_b[dy, dx, 0] = part[at : at + 2 * rows, half:].astype(bf16)


def grad_parts(place, logits, log_total, targets, scale, blocks):
    rows, cols = logits.shape
    width = blocks.shape[2]
    shape = (4, 4, 4, rows // 8, width // 2)
    whole = pl.BlockSpec((rows, cols), lambda i, place: (0, 0))
    column = pl.BlockSpec((rows, 1), lambda i, place: (0, 0))
    out = pl.BlockSpec((4, 4, 1, *shape[3:]), lambda i, place: (0, 0, i, 0, 0))
    return pl.pallas_call(
        grad_kernel,
        out_shape=[
            jax.ShapeDtypeStruct(shape, f32),
            jax.ShapeDtypeStruct(shape, f32),
            jax.ShapeDtypeStruct(shape, bf16),
            jax.ShapeDtypeStruct(shape, bf16),
        ],
        grid_spec=pltpu.PrefetchScalarGridSpec(
            num_scalar_prefetch=1,
            grid=(4,),
            in_specs=[whole, column, column, column, weight_spec(width, cols)],
            out_specs=[out, out, out, out],
            scratch_shapes=[pltpu.VMEM((rows, cols), f32)],
        ),
        compiler_params=pltpu.CompilerParams(dimension_semantics=("arbitrary",)),
        name="grad",
    )(place, logits, log_total[:, None], targets[:, None], scale[:, None], blocks)


def sent_to_all(shard, axis):
    copies = jnp.broadcast_to(shard, (lax.axis_size(axis), *shard.shape))
    return lax.all_to_all(copies, axis, split_axis=0, concat_axis=0, tiled=True)


def joined_all(stats, axes):
    for axis in axes:
        pieces = sent_to_all(stats, axis)
        peaks, totals, chosen = pieces[:, 0], pieces[:, 1], pieces[:, 2]
        peak = jnp.max(peaks, axis=0)
        total = jnp.sum(totals * jnp.exp(peaks - peak[None]), axis=0)
        stats = jnp.stack([peak, total, jnp.sum(chosen, axis=0)])
    return stats


def local(hidden, weight, targets, token_weight):
    rows_local, width = hidden.shape
    cols = weight.shape[1]
    px, pz, pc, ty, tz = (lax.axis_index(a) for a in AXES)
    section = px * 4 + pz * 2 + pc
    first_column = (section * 16 + ty * 4 + tz) * cols
    place = jnp.stack([px, pz, pc, ty, tz, first_column]).astype(jnp.int32)
    blocks = weight.reshape(4, 4, width, cols)
    scale = loss_scale * token_weight

    sections = []
    for k in range(4):
        same = hidden if k == 0 else along_z(hidden, 0, -k)
        sections.append(jnp.concatenate([same, along_z(hidden, 1, -k)], axis=0))
    sections = jnp.stack(sections)
    side_a = gathered_direct(sections[:, :, : width // 2], "ty")
    side_b = gathered_direct(sections[:, :, width // 2 :], "px")
    pieces = gathered_ring(side_a, "px") + gathered_ring(side_b, "ty")
    pieces = pieces + [shifted(p, "pc", 1) for p in pieces]
    logits = logits_of(place, pieces, blocks)

    columns = first_column + jnp.arange(cols, dtype=jnp.int32)
    target_hit = targets[:, None] == columns[None, :]
    chosen = jnp.sum(jnp.where(target_hit, logits, f32(0.0)), axis=1)
    local_peak = jnp.max(logits, axis=1)
    local_total = jnp.sum(jnp.exp(logits - local_peak[:, None]), axis=1)
    peak, total, target_logit = joined_all(
        jnp.stack([local_peak, local_total, chosen]), (PIPE, TENSOR)
    )
    log_total = peak + jnp.log(total)
    token_loss = lax.dynamic_slice_in_dim(
        log_total - target_logit, section * rows_local, rows_local, 0
    )

    keep_a, keep_b, send_a, send_b = grad_parts(place, logits, log_total, targets, scale, blocks)
    got_a = shifted(send_a, "pc", 1)
    got_b = shifted(send_b, "pc", 1)
    sums_a = reduced_ring(lambda k: keep_a[k] + got_a[k].astype(f32), "px")
    sums_b = reduced_ring(lambda k: keep_b[k] + got_b[k].astype(f32), "ty")
    left = jnp.concatenate(
        [reduced_direct(sums_a, "ty"), reduced_direct(sums_b, "px")], axis=2
    )
    grad = left[0, :rows_local]
    for flip in range(2):
        for k in range(4):
            if flip or k:
                part = left[k, flip * rows_local : (flip + 1) * rows_local]
                grad = grad + along_z(part, flip, k)
    return (token_loss, grad)


def solution(mesh):
    split = Mesh(mesh.devices.reshape(4, 2, 2, 4, 4), AXES)
    placed = (P(PIPE, TENSOR), P(None, PIPE + TENSOR), P(), P())
    return jax.shard_map(
        local, mesh=split, in_specs=placed, out_specs=(P(PIPE), P(PIPE, TENSOR)), check_vma=False
    )
```

```python
import jax
import jax.numpy as jnp
from jax import lax
from jax.experimental import pallas as pl
from jax.experimental.pallas import tpu as pltpu
from jax.sharding import Mesh
from jax.sharding import PartitionSpec as P

AXES = ("px", "pz", "pc", "ty", "tz")
PIPE = ("px", "pz", "pc")
TENSOR = ("ty", "tz")
DEPTH = ("pz", "tz")

loss_scale = 32.0
f32 = jnp.float32
bf16 = jnp.bfloat16


def shifted(block, axis, step):
    count = lax.axis_size(axis)
    return lax.ppermute(block, axis, [(i, (i + step) % count) for i in range(count)])


def sent_to_all(shard, axis):
    copies = jnp.broadcast_to(shard, (lax.axis_size(axis), *shard.shape))
    return lax.all_to_all(copies, axis, split_axis=0, concat_axis=0, tiled=True)


def exchanged(blocks, axis):
    return lax.all_to_all(blocks, axis, split_axis=0, concat_axis=0, tiled=True)


def gathered_direct(block, axis):
    return jnp.stack([block] + [shifted(block, axis, -k) for k in (1, 2, 3)])


def reduced_ring(own, axis):
    half = own[2].shape[0] // 2
    far = own[2].astype(bf16)
    far_first = shifted(far[:half], axis, 1).astype(f32)
    far_second = shifted(far[half:], axis, -1).astype(f32)
    after = jnp.concatenate([own[1][:half] + far_first, own[1][half:]]).astype(bf16)
    before = jnp.concatenate([own[3][:half], own[3][half:] + far_second]).astype(bf16)
    return own[0] + shifted(after, axis, 1).astype(f32) + shifted(before, axis, -1).astype(f32)


def reduced_direct(blocks, axis):
    total = blocks[0]
    for k in (1, 2, 3):
        total = total + shifted(blocks[k], axis, k)
    return total


def gathered_ring(block, axis):
    half = block.shape[1] // 2
    before = shifted(block, axis, 1)
    after = shifted(block, axis, -1)
    far_first = shifted(before[:, :half], axis, 1)
    far_second = shifted(after[:, half:], axis, -1)
    return [block, after, before, far_first, far_second]


def piece(refs, k, j, part, step):
    if k == 2:
        return refs[3 + part][j, step]
    return refs[{0: 0, 1: 1, 3: 2}[k]][j, 2 * part + step]


def weight_copies(w_ref, w_here, sems):
    return [pltpu.make_async_copy(w_ref.at[f], w_here.at[f], sems.at[f]) for f in range(16)]


def logits_kernel(place, *refs):
    a_refs = (refs[0:5], refs[10:15])
    b_refs = (refs[5:10], refs[15:20])
    w_ref, out_ref, lhs_ref, w_here, sems = refs[20:25]
    for copy in weight_copies(w_ref, w_here, sems):
        copy.start()
    px, pc, ty = place[0], place[2], place[3]
    rows, half = refs[0].shape[2], refs[0].shape[3]
    for part in range(2):

        @pl.loop(0, 2)
        def _(step, part=part):
            for dy in range(4):
                y = (ty + dy) % 4
                f = y * 4 + 2 * part + step
                for c in range(2):
                    for dx in range(4):
                        x = (px + dx) % 4
                        here = pl.ds(pl.multiple_of((((pc + c) % 2) * 4 + x) * rows, 16), rows)
                        lhs_ref[f, here, :half] = piece(a_refs[c], dx, y, part, step)
                        lhs_ref[f, here, half:] = piece(b_refs[c], dy, dx, part, step)

    def part_of(i):
        total = None
        for f in (2 * i, 2 * i + 1):
            pltpu.make_async_copy(w_ref.at[f], w_here.at[f], sems.at[f]).wait()
            part = jnp.dot(lhs_ref[f], w_here[f], preferred_element_type=f32)
            total = part if total is None else total + part
        return total

    out_ref[...] = part_of(0)

    @pl.loop(1, 8)
    def _(i):
        out_ref[...] += part_of(i)


def weight_scratch(blocks):
    return [pltpu.VMEM(blocks.shape, bf16), pltpu.SemaphoreType.DMA((16,))]


def on_chip():
    return pl.BlockSpec(memory_space=pltpu.VMEM)


def logits_of(place, pieces, blocks):
    rows, (_, width, cols) = pieces[0].shape[2] * 8, blocks.shape
    return pl.pallas_call(
        logits_kernel,
        out_shape=jax.ShapeDtypeStruct((rows, cols), f32),
        in_specs=[
            pl.BlockSpec(memory_space=pltpu.SMEM),
            *[on_chip()] * len(pieces),
            pl.BlockSpec(memory_space=pltpu.HBM),
        ],
        out_specs=on_chip(),
        scratch_shapes=[pltpu.VMEM((16, rows, width), bf16), *weight_scratch(blocks)],
        compiler_params=pltpu.CompilerParams(vmem_limit_bytes=20 << 20),
        name="logits",
    )(place, *[in_vmem(p) for p in pieces], blocks)


def grad_kernel(
    place, logits_ref, log_total_ref, targets_ref, scale_ref, w_ref, keep_a, keep_b, send_a, send_b, dl_ref, w_here, sems
):
    for copy in weight_copies(w_ref, w_here, sems):
        copy.start()
    cols = logits_ref.shape[1]
    rows, half = keep_a.shape[2], keep_a.shape[3]
    many = 4 * rows
    columns = place[5] + lax.broadcasted_iota(jnp.int32, (many, cols), 1)
    for c in range(2):
        here = pl.ds(pl.multiple_of(((place[2] + c) % 2) * many, 16), many)
        softmax = jnp.exp(logits_ref[here, :] - log_total_ref[here, :])
        hit = jnp.where(targets_ref[here, :] == columns, 1.0, 0.0)
        dl_ref[c * many : (c + 1) * many, :] = (scale_ref[here, :] * (softmax - hit)).astype(bf16)

    @pl.loop(0, 16)
    def _(f):
        pltpu.make_async_copy(w_ref.at[f], w_here.at[f], sems.at[f]).wait()
        part = lax.dot_general(
            dl_ref[...], w_here[f], (((1,), (1,)), ((), ())), preferred_element_type=f32
        )
        dy, z = (f // 4 + 4 - place[3]) % 4, f % 4
        g = dy * 4 + z
        for x in range(4):
            at = x * rows
            keep_a[x, g] = part[at : at + rows, :half]
            keep_b[dy, x * 4 + z] = part[at : at + rows, half:]
            at += many
            send_a[x, g] = part[at : at + rows, :half].astype(bf16)
            send_b[dy, x * 4 + z] = part[at : at + rows, half:].astype(bf16)


def grad_parts(place, logits, log_total, targets, scale, blocks):
    rows, cols = logits.shape
    shape = (4, 16, rows // 8, blocks.shape[1] // 2)
    return pl.pallas_call(
        grad_kernel,
        out_shape=[
            jax.ShapeDtypeStruct(shape, f32),
            jax.ShapeDtypeStruct(shape, f32),
            jax.ShapeDtypeStruct(shape, bf16),
            jax.ShapeDtypeStruct(shape, bf16),
        ],
        in_specs=[
            pl.BlockSpec(memory_space=pltpu.SMEM),
            *[on_chip()] * 4,
            pl.BlockSpec(memory_space=pltpu.HBM),
        ],
        out_specs=[on_chip()] * 4,
        scratch_shapes=[pltpu.VMEM((rows, cols), bf16), *weight_scratch(blocks)],
        compiler_params=pltpu.CompilerParams(vmem_limit_bytes=24 << 20),
        name="grad",
    )(place, logits, log_total[:, None], targets[:, None], scale[:, None], blocks)


def in_vmem(array):
    return pltpu.with_memory_space_constraint(array, pltpu.VMEM)


def joined_all(stats, axes):
    for axis in axes:
        pieces = sent_to_all(stats, axis)
        peaks, totals, chosen = pieces[:, 0], pieces[:, 1], pieces[:, 2]
        peak = jnp.max(peaks, axis=0)
        total = jnp.sum(totals * jnp.exp(peaks - peak[None]), axis=0)
        stats = jnp.stack([peak, total, jnp.sum(chosen, axis=0)])
    return stats


def by_core(rows):
    return rows.reshape(4, 2, 2, -1).transpose(2, 0, 1, 3).reshape(-1)


def local(hidden, weight, targets, token_weight):
    rows_local, width = hidden.shape
    cols = weight.shape[1]
    px, pz, pc, ty, tz = (lax.axis_index(a) for a in AXES)
    first_column = ((px * 4 + pz * 2 + pc) * 16 + ty * 4 + tz) * cols
    place = jnp.stack([px, pz, pc, ty, tz, first_column]).astype(jnp.int32)
    blocks = pltpu.with_memory_space_constraint(weight.reshape(16, width, cols), pltpu.HBM)
    targets = by_core(targets)
    scale = by_core(loss_scale * token_weight)
    half = width // 2

    sections = sent_to_all(hidden, DEPTH).reshape(2, 4, rows_local, width)
    sections = sections.transpose(1, 0, 2, 3).reshape(4, 2 * rows_local, width)
    side_a = sent_to_all(sections[:, :, :half], "ty")
    side_b = gathered_direct(sections[:, :, half:], "px")
    pieces = gathered_ring(side_a, "px") + gathered_ring(side_b, "ty")
    pieces = pieces + [shifted(p, "pc", 1) for p in pieces]
    logits = logits_of(place, pieces, blocks)

    columns = first_column + jnp.arange(cols, dtype=jnp.int32)
    target_hit = targets[:, None] == columns[None, :]
    chosen = jnp.sum(jnp.where(target_hit, logits, f32(0.0)), axis=1)
    local_peak = jnp.max(logits, axis=1)
    local_total = jnp.sum(jnp.exp(logits - local_peak[:, None]), axis=1)
    peak, total, target_logit = joined_all(
        jnp.stack([local_peak, local_total, chosen]), (PIPE, TENSOR)
    )
    log_total = peak + jnp.log(total)
    token_loss = lax.dynamic_slice_in_dim(
        log_total - target_logit, (pc * 8 + px * 2 + pz) * rows_local, rows_local, 0
    )

    keep_a, keep_b, send_a, send_b = grad_parts(place, logits, log_total, targets, scale, blocks)
    sum_a = keep_a + shifted(send_a, "pc", 1).astype(f32)
    sum_b = keep_b + shifted(send_b, "pc", 1).astype(f32)
    shape = (4, 4, 2 * rows_local, half)
    left_a = jnp.sum(exchanged(sum_a.astype(bf16), "px").astype(f32), axis=0).reshape(shape)
    left_b = reduced_ring(sum_b, "ty").reshape(shape)
    left_a = reduced_direct(left_a, "ty")
    left_b = jnp.sum(exchanged(left_b, "px"), axis=0)
    left = jnp.concatenate([left_a, left_b], axis=2)
    left = left.reshape(4, 2, rows_local, width).transpose(1, 0, 2, 3)
    left = left.reshape(8, rows_local, width)
    return (token_loss, jnp.sum(exchanged(left, DEPTH), axis=0))


def solution(mesh):
    split = Mesh(mesh.devices.reshape(4, 2, 2, 4, 4), AXES)
    placed = (P(PIPE, TENSOR), P(None, PIPE + TENSOR), P(), P())
    return jax.shard_map(
        local, mesh=split, in_specs=placed, out_specs=(P(PIPE), P(PIPE, TENSOR)), check_vma=False
    )
```

```python
import jax
import jax.numpy as jnp
from jax import lax
from jax.experimental import pallas as pl
from jax.experimental.pallas import tpu as pltpu
from jax.sharding import Mesh
from jax.sharding import PartitionSpec as P

AXES = ("px", "pz", "pc", "ty", "tz")
PIPE = ("px", "pz", "pc")
TENSOR = ("ty", "tz")
DEPTH = ("pz", "tz")
NEAR = ("px", "pz", "ty")

loss_scale = 32.0
f32 = jnp.float32
bf16 = jnp.bfloat16


def shifted(block, axis, step):
    count = lax.axis_size(axis)
    return lax.ppermute(block, axis, [(i, (i + step) % count) for i in range(count)])


def sent_to_all(shard, axis):
    copies = jnp.broadcast_to(shard, (lax.axis_size(axis), *shard.shape))
    return lax.all_to_all(copies, axis, split_axis=0, concat_axis=0, tiled=True)


def exchanged(blocks, axis):
    return lax.all_to_all(blocks, axis, split_axis=0, concat_axis=0, tiled=True)


def gathered_direct(block, axis):
    return jnp.stack([block] + [shifted(block, axis, -k) for k in (1, 2, 3)])


def gathered_ring(block, axis):
    half = block.shape[1] // 2
    before = shifted(block, axis, 1)
    after = shifted(block, axis, -1)
    far_first = shifted(before[:, :half], axis, 1)
    far_second = shifted(after[:, half:], axis, -1)
    return [block, after, before, far_first, far_second]


def piece(refs, k, j, part, step):
    if k == 2:
        return refs[3 + part][j, step]
    return refs[{0: 0, 1: 1, 3: 2}[k]][j, 2 * part + step]


def weight_copies(w_ref, w_here, sems):
    return [pltpu.make_async_copy(w_ref.at[f], w_here.at[f], sems.at[f]) for f in range(16)]


def logits_kernel(place, *refs):
    a_refs = (refs[0:5], refs[10:15])
    b_refs = (refs[5:10], refs[15:20])
    w_ref, out_ref, lhs_ref, w_here, sems = refs[20:25]
    for copy in weight_copies(w_ref, w_here, sems):
        copy.start()
    px, pc, ty = place[0], place[2], place[3]
    rows, half = refs[0].shape[2], refs[0].shape[3]
    for part in range(2):

        @pl.loop(0, 2)
        def _(step, part=part):
            for dy in range(4):
                y = (ty + dy) % 4
                f = y * 4 + 2 * part + step
                for c in range(2):
                    for dx in range(4):
                        x = (px + dx) % 4
                        here = pl.ds(pl.multiple_of((((pc + c) % 2) * 4 + x) * rows, 16), rows)
                        lhs_ref[f, here, :half] = piece(a_refs[c], dx, y, part, step)
                        lhs_ref[f, here, half:] = piece(b_refs[c], dy, dx, part, step)

    def part_of(i):
        total = None
        for f in (2 * i, 2 * i + 1):
            pltpu.make_async_copy(w_ref.at[f], w_here.at[f], sems.at[f]).wait()
            part = jnp.dot(lhs_ref[f], w_here[f], preferred_element_type=f32)
            total = part if total is None else total + part
        return total

    out_ref[...] = part_of(0)

    @pl.loop(1, 8)
    def _(i):
        out_ref[...] += part_of(i)


def weight_scratch(blocks):
    return [pltpu.VMEM(blocks.shape, bf16), pltpu.SemaphoreType.DMA((16,))]


def on_chip():
    return pl.BlockSpec(memory_space=pltpu.VMEM)


def logits_of(place, pieces, blocks):
    rows, (_, width, cols) = pieces[0].shape[2] * 8, blocks.shape
    return pl.pallas_call(
        logits_kernel,
        out_shape=jax.ShapeDtypeStruct((rows, cols), f32),
        in_specs=[
            pl.BlockSpec(memory_space=pltpu.SMEM),
            *[on_chip()] * len(pieces),
            pl.BlockSpec(memory_space=pltpu.HBM),
        ],
        out_specs=on_chip(),
        scratch_shapes=[pltpu.VMEM((16, rows, width), bf16), *weight_scratch(blocks)],
        compiler_params=pltpu.CompilerParams(vmem_limit_bytes=20 << 20),
        name="logits",
    )(place, *[in_vmem(p) for p in pieces], blocks)


def grad_kernel(
    place, logits_ref, log_total_ref, targets_ref, scale_ref, w_ref, keep, send, dl_ref, w_here, sems
):
    for copy in weight_copies(w_ref, w_here, sems):
        copy.start()
    cols = logits_ref.shape[1]
    rows = keep.shape[2]
    many = 8 * rows
    columns = place[5] + lax.broadcasted_iota(jnp.int32, (many, cols), 1)
    for c in range(2):
        here = pl.ds(pl.multiple_of(((place[2] + c) % 2) * many, 16), many)
        softmax = jnp.exp(logits_ref[here, :] - log_total_ref[here, :])
        hit = jnp.where(targets_ref[here, :] == columns, 1.0, 0.0)
        dl_ref[c * many : (c + 1) * many, :] = (scale_ref[here, :] * (softmax - hit)).astype(bf16)

    @pl.loop(0, 16)
    def _(f):
        pltpu.make_async_copy(w_ref.at[f], w_here.at[f], sems.at[f]).wait()
        part = lax.dot_general(
            dl_ref[...], w_here[f], (((1,), (1,)), ((), ())), preferred_element_type=f32
        )
        y, z = f // 4, f % 4
        for b in range(8):
            at = b * rows
            keep[b * 4 + y, z] = part[at : at + rows]
            send[b * 4 + y, z] = part[many + at : many + at + rows].astype(bf16)


def grad_parts(place, logits, log_total, targets, scale, blocks):
    rows, cols = logits.shape
    shape = (32, 4, rows // 16, blocks.shape[1])
    return pl.pallas_call(
        grad_kernel,
        out_shape=[
            jax.ShapeDtypeStruct(shape, f32),
            jax.ShapeDtypeStruct(shape, bf16),
        ],
        in_specs=[
            pl.BlockSpec(memory_space=pltpu.SMEM),
            *[on_chip()] * 4,
            pl.BlockSpec(memory_space=pltpu.HBM),
        ],
        out_specs=[on_chip()] * 2,
        scratch_shapes=[pltpu.VMEM((rows, cols), bf16), *weight_scratch(blocks)],
        compiler_params=pltpu.CompilerParams(vmem_limit_bytes=24 << 20),
        name="grad",
    )(place, logits, log_total[:, None], targets[:, None], scale[:, None], blocks)


def in_vmem(array):
    return pltpu.with_memory_space_constraint(array, pltpu.VMEM)


def joined_all(stats, axes):
    for axis in axes:
        pieces = sent_to_all(stats, axis)
        peaks, totals, chosen = pieces[:, 0], pieces[:, 1], pieces[:, 2]
        peak = jnp.max(peaks, axis=0)
        total = jnp.sum(totals * jnp.exp(peaks - peak[None]), axis=0)
        stats = jnp.stack([peak, total, jnp.sum(chosen, axis=0)])
    return stats


def by_core(rows):
    return rows.reshape(4, 2, 2, -1).transpose(2, 0, 1, 3).reshape(-1)


def local(hidden, weight, targets, token_weight):
    rows_local, width = hidden.shape
    cols = weight.shape[1]
    px, pz, pc, ty, tz = (lax.axis_index(a) for a in AXES)
    first_column = ((px * 4 + pz * 2 + pc) * 16 + ty * 4 + tz) * cols
    place = jnp.stack([px, pz, pc, ty, tz, first_column]).astype(jnp.int32)
    blocks = pltpu.with_memory_space_constraint(weight.reshape(16, width, cols), pltpu.HBM)
    targets = by_core(targets)
    scale = by_core(loss_scale * token_weight)
    half = width // 2

    sections = sent_to_all(hidden, DEPTH).reshape(2, 4, rows_local, width)
    sections = sections.transpose(1, 0, 2, 3).reshape(4, 2 * rows_local, width)
    side_a = sent_to_all(sections[:, :, :half], "ty")
    side_b = gathered_direct(sections[:, :, half:], "px")
    pieces = gathered_ring(side_a, "px") + gathered_ring(side_b, "ty")
    pieces = pieces + [shifted(p, "pc", 1) for p in pieces]
    logits = logits_of(place, pieces, blocks)

    columns = first_column + jnp.arange(cols, dtype=jnp.int32)
    target_hit = targets[:, None] == columns[None, :]
    chosen = jnp.sum(jnp.where(target_hit, logits, f32(0.0)), axis=1)
    local_peak = jnp.max(logits, axis=1)
    local_total = jnp.sum(jnp.exp(logits - local_peak[:, None]), axis=1)
    peak, total, target_logit = joined_all(
        jnp.stack([local_peak, local_total, chosen]), (("pz", "pc", "tz"), ("px", "ty"))
    )
    log_total = peak + jnp.log(total)
    token_loss = lax.dynamic_slice_in_dim(
        log_total - target_logit, (pc * 8 + px * 2 + pz) * rows_local, rows_local, 0
    )

    keep, send = grad_parts(place, logits, log_total, targets, scale, blocks)
    both = (keep + shifted(send, "pc", 1).astype(f32)).astype(bf16)
    left = jnp.sum(exchanged(both, NEAR).astype(f32), axis=0)
    return (token_loss, jnp.sum(exchanged(left, "tz"), axis=0))


def solution(mesh):
    split = Mesh(mesh.devices.reshape(4, 2, 2, 4, 4), AXES)
    placed = (P(PIPE, TENSOR), P(None, PIPE + TENSOR), P(), P())
    return jax.shard_map(
        local, mesh=split, in_specs=placed, out_specs=(P(PIPE), P(PIPE, TENSOR)), check_vma=False
    )
```

```python
import functools

import jax
import jax.numpy as jnp
from jax import lax
from jax.experimental import pallas as pl
from jax.experimental.pallas import tpu as pltpu
from jax.sharding import Mesh
from jax.sharding import PartitionSpec as P

AXES = ("px", "pz", "pc", "ty", "tz")
PIPE = ("px", "pz", "pc")
TENSOR = ("ty", "tz")
DEPTH = ("pz", "tz")
NEAR = ("px", "pz", "ty")

loss_scale = 32.0
f32 = jnp.float32
bf16 = jnp.bfloat16


def shifted(block, axis, step):
    count = lax.axis_size(axis)
    return lax.ppermute(block, axis, [(i, (i + step) % count) for i in range(count)])


def sent_to_all(shard, axis):
    copies = jnp.broadcast_to(shard, (lax.axis_size(axis), *shard.shape))
    return lax.all_to_all(copies, axis, split_axis=0, concat_axis=0, tiled=True)


def exchanged(blocks, axis):
    return lax.all_to_all(blocks, axis, split_axis=0, concat_axis=0, tiled=True)


def gathered_direct(block, axis):
    return jnp.stack([block] + [shifted(block, axis, -k) for k in (1, 2, 3)])


def gathered_ring(block, axis):
    half = block.shape[1] // 2
    before = shifted(block, axis, 1)
    after = shifted(block, axis, -1)
    far_first = shifted(before[:, :half], axis, 1)
    far_second = shifted(after[:, half:], axis, -1)
    return [in_vmem(p) for p in (block, after, before)] + [in_hbm(far_first), in_hbm(far_second)]


def piece(refs, k, j, part, step):
    if k == 2:
        return refs[3 + part][j, step]
    return refs[{0: 0, 1: 1, 3: 2}[k]][j, 2 * part + step]


def weight_copies(w_ref, w_here, sems):
    return [pltpu.make_async_copy(w_ref.at[f], w_here.at[f], sems.at[f]) for f in range(16)]


def stage_kernel(after_ref, w_ref, out_ref, sems):
    copies = weight_copies(w_ref, out_ref, sems)
    for copy in copies:
        copy.start()
    for copy in copies:
        copy.wait()


def staged(blocks, after):
    return pl.pallas_call(
        stage_kernel,
        out_shape=jax.ShapeDtypeStruct(blocks.shape, bf16),
        in_specs=[pl.BlockSpec(memory_space=pl.ANY), pl.BlockSpec(memory_space=pltpu.HBM)],
        out_specs=on_chip(),
        scratch_shapes=[pltpu.SemaphoreType.DMA((16,))],
        compiler_params=pltpu.CompilerParams(vmem_limit_bytes=1 << 20),
        cost_estimate=pl.CostEstimate(
            flops=0, transcendentals=0, bytes_accessed=2 * blocks.size * 2
        ),
        name="stage",
    )(after, blocks)


def logits_kernel(place, *refs):
    a_refs = (refs[0:5], refs[10:15])
    b_refs = (refs[5:10], refs[15:20])
    w_ref, out_ref, lhs_ref = refs[20:23]
    px, pc, ty = place[0], place[2], place[3]
    rows, half = refs[0].shape[2], refs[0].shape[3]
    for part in range(2):

        @pl.loop(0, 2)
        def _(step, part=part):
            for dy in range(4):
                y = (ty + dy) % 4
                f = y * 4 + 2 * part + step
                for c in range(2):
                    for dx in range(4):
                        x = (px + dx) % 4
                        here = pl.ds(pl.multiple_of((((pc + c) % 2) * 4 + x) * rows, 16), rows)
                        lhs_ref[f, here, :half] = piece(a_refs[c], dx, y, part, step)
                        lhs_ref[f, here, half:] = piece(b_refs[c], dy, dx, part, step)

    def part_of(i):
        total = None
        for f in (2 * i, 2 * i + 1):
            part = jnp.dot(lhs_ref[f], w_ref[f], preferred_element_type=f32)
            total = part if total is None else total + part
        return total

    out_ref[...] = part_of(0)

    @pl.loop(1, 8)
    def _(i):
        out_ref[...] += part_of(i)


def on_chip():
    return pl.BlockSpec(memory_space=pltpu.VMEM)


def logits_of(place, pieces, blocks):
    rows, (_, width, cols) = pieces[0].shape[2] * 8, blocks.shape
    return pl.pallas_call(
        logits_kernel,
        out_shape=jax.ShapeDtypeStruct((rows, cols), f32),
        in_specs=[
            pl.BlockSpec(memory_space=pltpu.SMEM),
            *[on_chip()] * (len(pieces) + 1),
        ],
        out_specs=on_chip(),
        scratch_shapes=[pltpu.VMEM((16, rows, width), bf16)],
        compiler_params=pltpu.CompilerParams(vmem_limit_bytes=12 << 20),
        name="logits",
    )(place, *pieces, blocks)


def grad_kernel(
    place, logits_ref, log_total_ref, targets_ref, scale_ref, w_ref, out_ref, dl_ref, w_here, sems, *, other
):
    for copy in weight_copies(w_ref, w_here, sems):
        copy.start()
    cols = logits_ref.shape[1]
    rows = out_ref.shape[2]
    many = 8 * rows
    columns = place[5] + lax.broadcasted_iota(jnp.int32, (many, cols), 1)
    here = pl.ds(pl.multiple_of(((place[2] + other) % 2) * many, 16), many)
    softmax = jnp.exp(logits_ref[here, :] - log_total_ref[here, :])
    hit = jnp.where(targets_ref[here, :] == columns, 1.0, 0.0)
    dl_ref[...] = (scale_ref[here, :] * (softmax - hit)).astype(bf16)

    @pl.loop(0, 16)
    def _(f):
        pltpu.make_async_copy(w_ref.at[f], w_here.at[f], sems.at[f]).wait()
        part = lax.dot_general(
            dl_ref[...], w_here[f], (((1,), (1,)), ((), ())), preferred_element_type=f32
        )
        y, z = f // 4, f % 4
        for b in range(8):
            out_ref[b * 4 + y, z] = part[b * rows : (b + 1) * rows].astype(out_ref.dtype)


def grad_part(place, logits, log_total, targets, scale, blocks, other, dtype):
    rows, cols = logits.shape
    shape = (32, 4, rows // 16, blocks.shape[1])
    return pl.pallas_call(
        functools.partial(grad_kernel, other=other),
        out_shape=jax.ShapeDtypeStruct(shape, dtype),
        in_specs=[
            pl.BlockSpec(memory_space=pltpu.SMEM),
            *[on_chip()] * 4,
            pl.BlockSpec(memory_space=pltpu.HBM),
        ],
        out_specs=on_chip(),
        scratch_shapes=[
            pltpu.VMEM((rows // 2, cols), bf16),
            pltpu.VMEM(blocks.shape, bf16),
            pltpu.SemaphoreType.DMA((16,)),
        ],
        compiler_params=pltpu.CompilerParams(vmem_limit_bytes=16 << 20),
        name="grad",
    )(place, logits, log_total[:, None], targets[:, None], scale[:, None], blocks)


def in_vmem(array):
    return pltpu.with_memory_space_constraint(array, pltpu.VMEM)


def in_hbm(array):
    return pltpu.with_memory_space_constraint(array, pltpu.HBM)


def joined(stats, axes):
    pieces = sent_to_all(stats, axes)
    peaks, totals, chosen = pieces[:, 0], pieces[:, 1], pieces[:, 2]
    peak = jnp.max(peaks, axis=0)
    total = jnp.sum(totals * jnp.exp(peaks - peak[None]), axis=0)
    return jnp.stack([peak, total, jnp.sum(chosen, axis=0)])


def by_core(rows):
    return rows.reshape(4, 2, 2, -1).transpose(2, 0, 1, 3).reshape(-1)


def local(hidden, weight, targets, token_weight):
    rows_local, width = hidden.shape
    cols = weight.shape[1]
    px, pz, pc, ty, tz = (lax.axis_index(a) for a in AXES)
    first_column = ((px * 4 + pz * 2 + pc) * 16 + ty * 4 + tz) * cols
    place = jnp.stack([px, pz, pc, ty, tz, first_column]).astype(jnp.int32)
    blocks = in_hbm(weight.reshape(16, width, cols))
    targets = by_core(targets)
    scale = by_core(loss_scale * token_weight)
    half = width // 2

    sections = sent_to_all(hidden, DEPTH).reshape(2, 4, rows_local, width)
    sections = sections.transpose(1, 0, 2, 3).reshape(4, 2 * rows_local, width)
    side_a = sent_to_all(sections[:, :, :half], "ty")
    side_b = gathered_direct(sections[:, :, half:], "px")
    pieces = gathered_ring(side_a, "px") + gathered_ring(side_b, "ty")
    weights = staged(blocks, pieces[2])
    pieces = pieces + [in_hbm(shifted(p, "pc", 1)) for p in pieces]
    logits = logits_of(place, pieces, weights)

    columns = first_column + jnp.arange(cols, dtype=jnp.int32)
    target_hit = targets[:, None] == columns[None, :]
    chosen = jnp.sum(jnp.where(target_hit, logits, f32(0.0)), axis=1)
    local_peak = jnp.max(logits, axis=1)
    local_total = jnp.sum(jnp.exp(logits - local_peak[:, None]), axis=1)
    stats = joined(jnp.stack([local_peak, local_total, chosen]), ("pz", "pc", "tz"))
    peak, total, target_logit = joined(stats, ("px", "ty"))
    log_total = peak + jnp.log(total)
    token_loss = lax.dynamic_slice_in_dim(
        log_total - target_logit, (pc * 8 + px * 2 + pz) * rows_local, rows_local, 0
    )

    terms = (place, logits, log_total, targets, scale, blocks)
    send = grad_part(*terms, 1, bf16)
    got = shifted(send, "pc", 1)
    keep = grad_part(*terms, 0, f32)
    both = (keep + got.astype(f32)).astype(bf16)
    left = jnp.sum(exchanged(both, NEAR).astype(f32), axis=0)
    return (token_loss, jnp.sum(exchanged(left, "tz"), axis=0))


def solution(mesh):
    split = Mesh(mesh.devices.reshape(4, 2, 2, 4, 4), AXES)
    placed = (P(PIPE, TENSOR), P(None, PIPE + TENSOR), P(), P())
    return jax.shard_map(
        local, mesh=split, in_specs=placed, out_specs=(P(PIPE), P(PIPE, TENSOR)), check_vma=False
    )
```

```python
import jax
import jax.numpy as jnp
from jax import lax
from jax.experimental import pallas as pl
from jax.experimental.pallas import tpu as pltpu
from jax.sharding import Mesh
from jax.sharding import PartitionSpec as P

AXES = ("px", "pz", "pc", "ty", "tz")
PIPE = ("px", "pz", "pc")
TENSOR = ("ty", "tz")
DEPTH = ("pz", "tz")
NEAR = ("px", "pz", "ty")

loss_scale = 32.0
f32 = jnp.float32
bf16 = jnp.bfloat16


def shifted(block, axis, step):
    count = lax.axis_size(axis)
    return lax.ppermute(block, axis, [(i, (i + step) % count) for i in range(count)])


def sent_to_all(shard, axis):
    copies = jnp.broadcast_to(shard, (lax.axis_size(axis), *shard.shape))
    return lax.all_to_all(copies, axis, split_axis=0, concat_axis=0, tiled=True)


def exchanged(blocks, axis):
    return lax.all_to_all(blocks, axis, split_axis=0, concat_axis=0, tiled=True)


def gathered_direct(block, axis):
    return jnp.stack([block] + [shifted(block, axis, -k) for k in (1, 2, 3)])


def gathered_ring(block, axis):
    half = block.shape[1] // 2
    before = shifted(block, axis, 1)
    after = shifted(block, axis, -1)
    far_first = shifted(before[:, :half], axis, 1)
    far_second = shifted(after[:, half:], axis, -1)
    return [in_vmem(p) for p in (block, after, before)] + [in_hbm(far_first), in_hbm(far_second)]


def piece(refs, k, j, part, step):
    if k == 2:
        return refs[3 + part][j, step]
    return refs[{0: 0, 1: 1, 3: 2}[k]][j, 2 * part + step]


def weight_copies(w_ref, w_here, sems, which):
    return [pltpu.make_async_copy(w_ref.at[f], w_here.at[f], sems.at[f]) for f in which]


def logits_kernel(place, *refs):
    a_refs = (refs[0:5], refs[10:15])
    b_refs = (refs[5:10], refs[15:20])
    w_ref, out_ref = refs[20:22]
    lhs_refs, w_here, sems = refs[22:26], refs[26], refs[27]
    px, pc, ty = place[0], place[2], place[3]
    order = [(ty + dy) % 4 * 4 + z for z in range(4) for dy in range(4)]
    for copy in weight_copies(w_ref, w_here, sems, order):
        copy.start()
    rows, half = refs[0].shape[2], refs[0].shape[3]

    def part_of(part, step):
        total = None
        for dy in range(4):
            y = (ty + dy) % 4
            f = y * 4 + 2 * part + step
            lhs_ref = lhs_refs[dy]
            for c in range(2):
                for dx in range(4):
                    x = (px + dx) % 4
                    here = pl.ds(pl.multiple_of((((pc + c) % 2) * 4 + x) * rows, 16), rows)
                    lhs_ref[here, :half] = piece(a_refs[c], dx, y, part, step)
                    lhs_ref[here, half:] = piece(b_refs[c], dy, dx, part, step)
            pltpu.make_async_copy(w_ref.at[f], w_here.at[f], sems.at[f]).wait()
            term = jnp.dot(lhs_ref[...], w_here[f], preferred_element_type=f32)
            total = term if total is None else total + term
        return total

    out_ref[...] = jnp.zeros_like(out_ref)
    for part in range(2):

        @pl.loop(0, 2)
        def _(step, part=part):
            out_ref[...] += part_of(part, step)


def weight_scratch(blocks):
    return [pltpu.VMEM(blocks.shape, bf16), pltpu.SemaphoreType.DMA((16,))]


def on_chip():
    return pl.BlockSpec(memory_space=pltpu.VMEM)


def logits_of(place, pieces, blocks):
    rows, (_, width, cols) = pieces[0].shape[2] * 8, blocks.shape
    return pl.pallas_call(
        logits_kernel,
        out_shape=jax.ShapeDtypeStruct((rows, cols), f32),
        in_specs=[
            pl.BlockSpec(memory_space=pltpu.SMEM),
            *[on_chip()] * len(pieces),
            pl.BlockSpec(memory_space=pltpu.HBM),
        ],
        out_specs=on_chip(),
        scratch_shapes=[pltpu.VMEM((rows, width), bf16)] * 4 + weight_scratch(blocks),
        compiler_params=pltpu.CompilerParams(vmem_limit_bytes=20 << 20),
        name="logits",
    )(place, *pieces, blocks)


def grad_blocks(dlogits, w_ref, keep, send, w_here, sems, first):
    rows, count = keep.shape[3], keep.shape[1] * 4
    many = 8 * rows

    @pl.loop(0, count)
    def _(i):
        f = first + i
        pltpu.make_async_copy(w_ref.at[f], w_here.at[f], sems.at[f]).wait()
        part = lax.dot_general(
            dlogits[...], w_here[f], (((1,), (1,)), ((), ())), preferred_element_type=f32
        )
        y, z = i // 4, i % 4
        for b in range(8):
            at = b * rows
            keep[b, y, z] = part[at : at + rows]
            send[b, y, z] = part[many + at : many + at + rows].astype(bf16)


def grad_first_kernel(
    place, logits_ref, log_total_ref, targets_ref, scale_ref, w_ref, keep, send, dlogits, w_here, sems
):
    for copy in weight_copies(w_ref, w_here, sems, range(8)):
        copy.start()
    many, cols = dlogits.shape[0] // 2, dlogits.shape[1]
    columns = place[5] + lax.broadcasted_iota(jnp.int32, (many, cols), 1)
    for c in range(2):
        here = pl.ds(pl.multiple_of(((place[2] + c) % 2) * many, 16), many)
        softmax = jnp.exp(logits_ref[here, :] - log_total_ref[here, :])
        hit = jnp.where(targets_ref[here, :] == columns, 1.0, 0.0)
        dlogits[c * many : (c + 1) * many, :] = (scale_ref[here, :] * (softmax - hit)).astype(bf16)
    grad_blocks(dlogits, w_ref, keep, send, w_here, sems, 0)


def grad_second_kernel(dlogits, w_ref, keep, send, w_here, sems):
    for copy in weight_copies(w_ref, w_here, sems, range(8, 16)):
        copy.start()
    grad_blocks(dlogits, w_ref, keep, send, w_here, sems, 8)


def grad_parts(place, logits, log_total, targets, scale, blocks):
    rows, cols = logits.shape
    shape = (8, 2, 4, rows // 16, blocks.shape[1])
    outs = [
        jax.ShapeDtypeStruct(shape, f32),
        jax.ShapeDtypeStruct(shape, bf16),
        jax.ShapeDtypeStruct((rows, cols), bf16),
    ]
    params = pltpu.CompilerParams(vmem_limit_bytes=16 << 20)
    weights = pl.BlockSpec(memory_space=pltpu.HBM)
    keep, send, dlogits = pl.pallas_call(
        grad_first_kernel,
        out_shape=outs,
        in_specs=[pl.BlockSpec(memory_space=pltpu.SMEM), *[on_chip()] * 4, weights],
        out_specs=[on_chip()] * 3,
        scratch_shapes=weight_scratch(blocks),
        compiler_params=params,
        name="grad_first",
    )(place, logits, log_total[:, None], targets[:, None], scale[:, None], blocks)
    keep_more, send_more = pl.pallas_call(
        grad_second_kernel,
        out_shape=outs[:2],
        in_specs=[on_chip(), weights],
        out_specs=[on_chip()] * 2,
        scratch_shapes=weight_scratch(blocks),
        compiler_params=params,
        name="grad_second",
    )(dlogits, blocks)
    return (keep, keep_more), (send, send_more)


def in_vmem(array):
    return pltpu.with_memory_space_constraint(array, pltpu.VMEM)


def in_hbm(array):
    return pltpu.with_memory_space_constraint(array, pltpu.HBM)


def joined_all(stats, axes):
    for axis in axes:
        pieces = sent_to_all(stats, axis)
        peaks, totals, chosen = pieces[:, 0], pieces[:, 1], pieces[:, 2]
        peak = jnp.max(peaks, axis=0)
        total = jnp.sum(totals * jnp.exp(peaks - peak[None]), axis=0)
        stats = jnp.stack([peak, total, jnp.sum(chosen, axis=0)])
    return stats


def by_core(rows):
    return rows.reshape(4, 2, 2, -1).transpose(2, 0, 1, 3).reshape(-1)


def local(hidden, weight, targets, token_weight):
    rows_local, width = hidden.shape
    cols = weight.shape[1]
    px, pz, pc, ty, tz = (lax.axis_index(a) for a in AXES)
    first_column = ((px * 4 + pz * 2 + pc) * 16 + ty * 4 + tz) * cols
    place = jnp.stack([px, pz, pc, ty, tz, first_column]).astype(jnp.int32)
    blocks = in_hbm(weight.reshape(16, width, cols))
    targets = by_core(targets)
    scale = by_core(loss_scale * token_weight)
    half = width // 2

    sections = sent_to_all(hidden, DEPTH).reshape(2, 4, rows_local, width)
    sections = sections.transpose(1, 0, 2, 3).reshape(4, 2 * rows_local, width)
    side_a = sent_to_all(sections[:, :, :half], "ty")
    side_b = gathered_direct(sections[:, :, half:], "px")
    pieces = gathered_ring(side_a, "px") + gathered_ring(side_b, "ty")
    pieces = pieces + [in_hbm(shifted(p, "pc", 1)) for p in pieces]
    logits = logits_of(place, pieces, blocks)

    columns = first_column + jnp.arange(cols, dtype=jnp.int32)
    target_hit = targets[:, None] == columns[None, :]
    chosen = jnp.sum(jnp.where(target_hit, logits, f32(0.0)), axis=1)
    local_peak = jnp.max(logits, axis=1)
    local_total = jnp.sum(jnp.exp(logits - local_peak[:, None]), axis=1)
    peak, total, target_logit = joined_all(
        jnp.stack([local_peak, local_total, chosen]), (("pz", "pc", "tz"), ("px", "ty"))
    )
    log_total = peak + jnp.log(total)
    token_loss = lax.dynamic_slice_in_dim(
        log_total - target_logit, (pc * 8 + px * 2 + pz) * rows_local, rows_local, 0
    )

    keep, send = grad_parts(place, logits, log_total, targets, scale, blocks)
    both = [(k + shifted(s, "pc", 1).astype(f32)).astype(bf16) for k, s in zip(keep, send)]
    both = jnp.concatenate(both, axis=1).reshape(32, 4, rows_local, width)
    left = jnp.sum(exchanged(both, NEAR).astype(f32), axis=0)
    return (token_loss, jnp.sum(exchanged(left, "tz"), axis=0))


def solution(mesh):
    split = Mesh(mesh.devices.reshape(4, 2, 2, 4, 4), AXES)
    placed = (P(PIPE, TENSOR), P(None, PIPE + TENSOR), P(), P())
    return jax.shard_map(
        local, mesh=split, in_specs=placed, out_specs=(P(PIPE), P(PIPE, TENSOR)), check_vma=False
    )
```

```python
import jax
import jax.numpy as jnp
from jax import lax
from jax.experimental import pallas as pl
from jax.experimental.pallas import tpu as pltpu
from jax.sharding import Mesh
from jax.sharding import PartitionSpec as P

AXES = ("px", "pz", "pc", "ty", "tz")
PIPE = ("px", "pz", "pc")
TENSOR = ("ty", "tz")
DEPTH = ("pz", "tz")
NEAR = ("px", "pz", "ty")

loss_scale = 32.0
f32 = jnp.float32
bf16 = jnp.bfloat16


def shifted(block, axis, step):
    count = lax.axis_size(axis)
    return lax.ppermute(block, axis, [(i, (i + step) % count) for i in range(count)])


def sent_to_all(shard, axis):
    copies = jnp.broadcast_to(shard, (lax.axis_size(axis), *shard.shape))
    return lax.all_to_all(copies, axis, split_axis=0, concat_axis=0, tiled=True)


def exchanged(blocks, axis):
    return lax.all_to_all(blocks, axis, split_axis=0, concat_axis=0, tiled=True)


def gathered_direct(block, axis):
    return jnp.stack([block] + [shifted(block, axis, -k) for k in (1, 2, 3)])


def reduced_direct(blocks, axis):
    total = blocks[0]
    for k in (1, 2, 3):
        total = total + shifted(blocks[k], axis, k)
    return total


def gathered_ring(block, axis):
    half = block.shape[1] // 2
    before = shifted(block, axis, 1)
    after = shifted(block, axis, -1)
    far_first = shifted(before[:, :half], axis, 1)
    far_second = shifted(after[:, half:], axis, -1)
    return [in_vmem(p) for p in (block, after, before)] + [in_hbm(far_first), in_hbm(far_second)]


def piece(refs, k, j, part, step):
    if k == 2:
        return refs[3 + part][j, step]
    return refs[{0: 0, 1: 1, 3: 2}[k]][j, 2 * part + step]


def weight_copies(w_ref, w_here, sems, which):
    return [pltpu.make_async_copy(w_ref.at[f], w_here.at[f], sems.at[f]) for f in which]


def logits_kernel(place, *refs):
    a_refs = (refs[0:5], refs[10:15])
    b_refs = (refs[5:10], refs[15:20])
    w_ref, out_ref = refs[20:22]
    lhs_refs, w_here, sems = refs[22:26], refs[26], refs[27]
    px, pc, ty = place[0], place[2], place[3]
    order = [(ty + dy) % 4 * 4 + z for z in range(4) for dy in range(4)]
    for copy in weight_copies(w_ref, w_here, sems, order):
        copy.start()
    rows, half = refs[0].shape[2], refs[0].shape[3]

    def part_of(part, step):
        total = None
        for dy in range(4):
            y = (ty + dy) % 4
            f = y * 4 + 2 * part + step
            lhs_ref = lhs_refs[dy]
            for c in range(2):
                for dx in range(4):
                    x = (px + dx) % 4
                    here = pl.ds(pl.multiple_of((((pc + c) % 2) * 4 + x) * rows, 16), rows)
                    lhs_ref[here, :half] = piece(a_refs[c], dx, dy, part, step)
                    lhs_ref[here, half:] = piece(b_refs[c], dy, dx, part, step)
            pltpu.make_async_copy(w_ref.at[f], w_here.at[f], sems.at[f]).wait()
            term = jnp.dot(lhs_ref[...], w_here[f], preferred_element_type=f32)
            total = term if total is None else total + term
        return total

    out_ref[...] = jnp.zeros_like(out_ref)
    for part in range(2):

        @pl.loop(0, 2)
        def _(step, part=part):
            out_ref[...] += part_of(part, step)


def weight_scratch(blocks):
    return [pltpu.VMEM(blocks.shape, bf16), pltpu.SemaphoreType.DMA((16,))]


def on_chip():
    return pl.BlockSpec(memory_space=pltpu.VMEM)


def logits_of(place, pieces, blocks):
    rows, (_, width, cols) = pieces[0].shape[2] * 8, blocks.shape
    return pl.pallas_call(
        logits_kernel,
        out_shape=jax.ShapeDtypeStruct((rows, cols), f32),
        in_specs=[
            pl.BlockSpec(memory_space=pltpu.SMEM),
            *[on_chip()] * len(pieces),
            pl.BlockSpec(memory_space=pltpu.HBM),
        ],
        out_specs=on_chip(),
        scratch_shapes=[pltpu.VMEM((rows, width), bf16)] * 4 + weight_scratch(blocks),
        compiler_params=pltpu.CompilerParams(vmem_limit_bytes=20 << 20),
        name="logits",
    )(place, *pieces, blocks)


def grad_blocks(place, dlogits, w_ref, keep, send, w_here, sems, first):
    rows, count = keep.shape[3], keep.shape[1] * 4
    many = 8 * rows

    @pl.loop(0, count)
    def _(i):
        f = first + i
        pltpu.make_async_copy(w_ref.at[f], w_here.at[f], sems.at[f]).wait()
        part = lax.dot_general(
            dlogits[...], w_here[f], (((1,), (1,)), ((), ())), preferred_element_type=f32
        )
        y, z = i // 4, (i % 4 + 4 - place[4]) % 4
        for b in range(8):
            at = b * rows
            keep[b, y, z] = part[at : at + rows]
            send[b, y, z] = part[many + at : many + at + rows].astype(bf16)


def grad_first_kernel(
    place, logits_ref, log_total_ref, targets_ref, scale_ref, w_ref, keep, send, dlogits, w_here, sems
):
    for copy in weight_copies(w_ref, w_here, sems, range(8)):
        copy.start()
    many, cols = dlogits.shape[0] // 2, dlogits.shape[1]
    columns = place[5] + lax.broadcasted_iota(jnp.int32, (many, cols), 1)
    for c in range(2):
        here = pl.ds(pl.multiple_of(((place[2] + c) % 2) * many, 16), many)
        softmax = jnp.exp(logits_ref[here, :] - log_total_ref[here, :])
        hit = jnp.where(targets_ref[here, :] == columns, 1.0, 0.0)
        dlogits[c * many : (c + 1) * many, :] = (scale_ref[here, :] * (softmax - hit)).astype(bf16)
    grad_blocks(place, dlogits, w_ref, keep, send, w_here, sems, 0)


def grad_second_kernel(place, dlogits, w_ref, keep, send, w_here, sems):
    for copy in weight_copies(w_ref, w_here, sems, range(8, 16)):
        copy.start()
    grad_blocks(place, dlogits, w_ref, keep, send, w_here, sems, 8)


def grad_parts(place, logits, log_total, targets, scale, blocks):
    rows, cols = logits.shape
    shape = (8, 2, 4, rows // 16, blocks.shape[1])
    outs = [
        jax.ShapeDtypeStruct(shape, f32),
        jax.ShapeDtypeStruct(shape, bf16),
        jax.ShapeDtypeStruct((rows, cols), bf16),
    ]
    params = pltpu.CompilerParams(vmem_limit_bytes=16 << 20)
    weights = pl.BlockSpec(memory_space=pltpu.HBM)
    keep, send, dlogits = pl.pallas_call(
        grad_first_kernel,
        out_shape=outs,
        in_specs=[pl.BlockSpec(memory_space=pltpu.SMEM), *[on_chip()] * 4, weights],
        out_specs=[on_chip()] * 3,
        scratch_shapes=weight_scratch(blocks),
        compiler_params=params,
        name="grad_first",
    )(place, logits, log_total[:, None], targets[:, None], scale[:, None], blocks)
    keep_more, send_more = pl.pallas_call(
        grad_second_kernel,
        out_shape=outs[:2],
        in_specs=[pl.BlockSpec(memory_space=pltpu.SMEM), on_chip(), weights],
        out_specs=[on_chip()] * 2,
        scratch_shapes=weight_scratch(blocks),
        compiler_params=params,
        name="grad_second",
    )(place, dlogits, blocks)
    return (keep, keep_more), (send, send_more)


def in_vmem(array):
    return pltpu.with_memory_space_constraint(array, pltpu.VMEM)


def in_hbm(array):
    return pltpu.with_memory_space_constraint(array, pltpu.HBM)


def joined_all(stats, axes):
    for axis in axes:
        pieces = sent_to_all(stats, axis)
        peaks, totals, chosen = pieces[:, 0], pieces[:, 1], pieces[:, 2]
        peak = jnp.max(peaks, axis=0)
        total = jnp.sum(totals * jnp.exp(peaks - peak[None]), axis=0)
        stats = jnp.stack([peak, total, jnp.sum(chosen, axis=0)])
    return stats


def by_core(rows):
    return rows.reshape(4, 2, 2, -1).transpose(2, 0, 1, 3).reshape(-1)


def local(hidden, weight, targets, token_weight):
    rows_local, width = hidden.shape
    cols = weight.shape[1]
    px, pz, pc, ty, tz = (lax.axis_index(a) for a in AXES)
    first_column = ((px * 4 + pz * 2 + pc) * 16 + ty * 4 + tz) * cols
    place = jnp.stack([px, pz, pc, ty, tz, first_column]).astype(jnp.int32)
    blocks = in_hbm(weight.reshape(16, width, cols))
    targets = by_core(targets)
    scale = by_core(loss_scale * token_weight)
    half = width // 2

    sections = sent_to_all(hidden, DEPTH).reshape(2, 4, rows_local, width)
    sections = sections.transpose(1, 0, 2, 3).reshape(4, 2 * rows_local, width)
    side_a = gathered_direct(sections[:, :, :half], "ty")
    side_b = gathered_direct(sections[:, :, half:], "px")
    pieces = gathered_ring(side_a, "px") + gathered_ring(side_b, "ty")
    pieces = pieces + [in_hbm(shifted(p, "pc", 1)) for p in pieces]
    logits = logits_of(place, pieces, blocks)

    columns = first_column + jnp.arange(cols, dtype=jnp.int32)
    target_hit = targets[:, None] == columns[None, :]
    chosen = jnp.sum(jnp.where(target_hit, logits, f32(0.0)), axis=1)
    local_peak = jnp.max(logits, axis=1)
    local_total = jnp.sum(jnp.exp(logits - local_peak[:, None]), axis=1)
    peak, total, target_logit = joined_all(
        jnp.stack([local_peak, local_total, chosen]), (("pz", "pc", "tz"), ("px", "ty"))
    )
    log_total = peak + jnp.log(total)
    token_loss = lax.dynamic_slice_in_dim(
        log_total - target_logit, (pc * 8 + px * 2 + pz) * rows_local, rows_local, 0
    )

    keep, send = grad_parts(place, logits, log_total, targets, scale, blocks)
    both = [(k + shifted(s, "pc", 1).astype(f32)).astype(bf16) for k, s in zip(keep, send)]
    both = jnp.concatenate(both, axis=1).reshape(32, 4, rows_local, width)
    left = jnp.sum(exchanged(both, NEAR).astype(f32), axis=0)
    return (token_loss, reduced_direct(left, "tz"))


def solution(mesh):
    split = Mesh(mesh.devices.reshape(4, 2, 2, 4, 4), AXES)
    placed = (P(PIPE, TENSOR), P(None, PIPE + TENSOR), P(), P())
    return jax.shard_map(
        local, mesh=split, in_specs=placed, out_specs=(P(PIPE), P(PIPE, TENSOR)), check_vma=False
    )
```

```python
import jax
import jax.numpy as jnp
from jax import lax
from jax.experimental import pallas as pl
from jax.experimental.pallas import tpu as pltpu
from jax.sharding import Mesh
from jax.sharding import PartitionSpec as P

AXES = ("px", "pz", "pc", "ty", "tz")
PIPE = ("px", "pz", "pc")
TENSOR = ("ty", "tz")
DEPTH = ("pz", "tz")
NEAR = ("px", "pz", "ty")

loss_scale = 32.0
f32 = jnp.float32
bf16 = jnp.bfloat16


def shifted(block, axis, step):
    count = lax.axis_size(axis)
    return lax.ppermute(block, axis, [(i, (i + step) % count) for i in range(count)])


def sent_to_all(shard, axis):
    copies = jnp.broadcast_to(shard, (lax.axis_size(axis), *shard.shape))
    return lax.all_to_all(copies, axis, split_axis=0, concat_axis=0, tiled=True)


def exchanged(blocks, axis):
    return lax.all_to_all(blocks, axis, split_axis=0, concat_axis=0, tiled=True)


def gathered_direct(block, axis):
    return jnp.stack([block] + [shifted(block, axis, -k) for k in (1, 2, 3)])


def reduced_direct(blocks, axis):
    far = shifted(blocks[2].astype(bf16), axis, 2).astype(f32)
    return blocks[0] + shifted(blocks[1], axis, 1) + shifted(blocks[3], axis, 3) + far


def gathered_ring(block, axis):
    half = block.shape[1] // 2
    before = shifted(block, axis, 1)
    after = shifted(block, axis, -1)
    far_first = shifted(before[:, :half], axis, 1)
    far_second = shifted(after[:, half:], axis, -1)
    return [in_vmem(p) for p in (block, after, before)] + [in_hbm(far_first), in_hbm(far_second)]


def piece(refs, k, j, part, step):
    if k == 2:
        return refs[3 + part][j, step]
    return refs[{0: 0, 1: 1, 3: 2}[k]][j, 2 * part + step]


def weight_copies(w_ref, w_here, sems, which):
    return [pltpu.make_async_copy(w_ref.at[f], w_here.at[f], sems.at[f]) for f in which]


def logits_kernel(place, *refs):
    a_refs = (refs[0:5], refs[10:15])
    b_refs = (refs[5:10], refs[15:20])
    w_ref, out_ref = refs[20:22]
    lhs_refs, w_here, sems = refs[22:26], refs[26], refs[27]
    px, pc, ty = place[0], place[2], place[3]
    order = [(ty + dy) % 4 * 4 + z for z in range(4) for dy in range(4)]
    for copy in weight_copies(w_ref, w_here, sems, order):
        copy.start()
    rows, half = refs[0].shape[2], refs[0].shape[3]

    def part_of(part, step):
        total = None
        for dy in range(4):
            y = (ty + dy) % 4
            f = y * 4 + 2 * part + step
            lhs_ref = lhs_refs[dy]
            for c in range(2):
                for dx in range(4):
                    x = (px + dx) % 4
                    here = pl.ds(pl.multiple_of((((pc + c) % 2) * 4 + x) * rows, 16), rows)
                    lhs_ref[here, :half] = piece(a_refs[c], dx, dy, part, step)
                    lhs_ref[here, half:] = piece(b_refs[c], dy, dx, part, step)
            pltpu.make_async_copy(w_ref.at[f], w_here.at[f], sems.at[f]).wait()
            term = jnp.dot(lhs_ref[...], w_here[f], preferred_element_type=f32)
            total = term if total is None else total + term
        return total

    out_ref[...] = jnp.zeros_like(out_ref)
    for part in range(2):

        @pl.loop(0, 2)
        def _(step, part=part):
            out_ref[...] += part_of(part, step)


def weight_scratch(blocks):
    return [pltpu.VMEM(blocks.shape, bf16), pltpu.SemaphoreType.DMA((16,))]


def on_chip():
    return pl.BlockSpec(memory_space=pltpu.VMEM)


def logits_of(place, pieces, blocks):
    rows, (_, width, cols) = pieces[0].shape[2] * 8, blocks.shape
    return pl.pallas_call(
        logits_kernel,
        out_shape=jax.ShapeDtypeStruct((rows, cols), f32),
        in_specs=[
            pl.BlockSpec(memory_space=pltpu.SMEM),
            *[on_chip()] * len(pieces),
            pl.BlockSpec(memory_space=pltpu.HBM),
        ],
        out_specs=on_chip(),
        scratch_shapes=[pltpu.VMEM((rows, width), bf16)] * 4 + weight_scratch(blocks),
        compiler_params=pltpu.CompilerParams(vmem_limit_bytes=20 << 20),
        name="logits",
    )(place, *pieces, blocks)


def grad_blocks(place, dlogits, w_ref, keep, send, w_here, sems, first):
    rows, count = keep.shape[3], keep.shape[1] * 4
    many = 8 * rows

    @pl.loop(0, count)
    def _(i):
        f = first + i
        pltpu.make_async_copy(w_ref.at[f], w_here.at[f], sems.at[f]).wait()
        part = lax.dot_general(
            dlogits[...], w_here[f], (((1,), (1,)), ((), ())), preferred_element_type=f32
        )
        y, z = i // 4, (i % 4 + 4 - place[4]) % 4
        for b in range(8):
            at = b * rows
            keep[b, y, z] = part[at : at + rows]
            send[b, y, z] = part[many + at : many + at + rows].astype(bf16)


def grad_first_kernel(
    place, logits_ref, log_total_ref, targets_ref, scale_ref, w_ref, keep, send, dlogits, w_here, sems
):
    for copy in weight_copies(w_ref, w_here, sems, range(8)):
        copy.start()
    many, cols = dlogits.shape[0] // 2, dlogits.shape[1]
    columns = place[5] + lax.broadcasted_iota(jnp.int32, (many, cols), 1)
    for c in range(2):
        here = pl.ds(pl.multiple_of(((place[2] + c) % 2) * many, 16), many)
        softmax = jnp.exp(logits_ref[here, :] - log_total_ref[here, :])
        hit = jnp.where(targets_ref[here, :] == columns, 1.0, 0.0)
        dlogits[c * many : (c + 1) * many, :] = (scale_ref[here, :] * (softmax - hit)).astype(bf16)
    grad_blocks(place, dlogits, w_ref, keep, send, w_here, sems, 0)


def grad_second_kernel(place, dlogits, w_ref, keep, send, w_here, sems):
    for copy in weight_copies(w_ref, w_here, sems, range(8, 16)):
        copy.start()
    grad_blocks(place, dlogits, w_ref, keep, send, w_here, sems, 8)


def grad_parts(place, logits, log_total, targets, scale, blocks):
    rows, cols = logits.shape
    shape = (8, 2, 4, rows // 16, blocks.shape[1])
    outs = [
        jax.ShapeDtypeStruct(shape, f32),
        jax.ShapeDtypeStruct(shape, bf16),
        jax.ShapeDtypeStruct((rows, cols), bf16),
    ]
    params = pltpu.CompilerParams(vmem_limit_bytes=16 << 20)
    weights = pl.BlockSpec(memory_space=pltpu.HBM)
    keep, send, dlogits = pl.pallas_call(
        grad_first_kernel,
        out_shape=outs,
        in_specs=[pl.BlockSpec(memory_space=pltpu.SMEM), *[on_chip()] * 4, weights],
        out_specs=[on_chip()] * 3,
        scratch_shapes=weight_scratch(blocks),
        compiler_params=params,
        name="grad_first",
    )(place, logits, log_total[:, None], targets[:, None], scale[:, None], blocks)
    keep_more, send_more = pl.pallas_call(
        grad_second_kernel,
        out_shape=outs[:2],
        in_specs=[pl.BlockSpec(memory_space=pltpu.SMEM), on_chip(), weights],
        out_specs=[on_chip()] * 2,
        scratch_shapes=weight_scratch(blocks),
        compiler_params=params,
        name="grad_second",
    )(place, dlogits, blocks)
    return (keep, keep_more), (send, send_more)


def in_vmem(array):
    return pltpu.with_memory_space_constraint(array, pltpu.VMEM)


def in_hbm(array):
    return pltpu.with_memory_space_constraint(array, pltpu.HBM)


def joined_all(stats, axes):
    for axis in axes:
        pieces = sent_to_all(stats, axis)
        peaks, totals, chosen = pieces[:, 0], pieces[:, 1], pieces[:, 2]
        peak = jnp.max(peaks, axis=0)
        total = jnp.sum(totals * jnp.exp(peaks - peak[None]), axis=0)
        stats = jnp.stack([peak, total, jnp.sum(chosen, axis=0)])
    return stats


def by_core(rows):
    return rows.reshape(4, 2, 2, -1).transpose(2, 0, 1, 3).reshape(-1)


def local(hidden, weight, targets, token_weight):
    rows_local, width = hidden.shape
    cols = weight.shape[1]
    px, pz, pc, ty, tz = (lax.axis_index(a) for a in AXES)
    first_column = ((px * 4 + pz * 2 + pc) * 16 + ty * 4 + tz) * cols
    place = jnp.stack([px, pz, pc, ty, tz, first_column]).astype(jnp.int32)
    blocks = in_hbm(weight.reshape(16, width, cols))
    targets = by_core(targets)
    scale = by_core(loss_scale * token_weight)
    half = width // 2

    sections = sent_to_all(hidden, DEPTH).reshape(2, 4, rows_local, width)
    sections = sections.transpose(1, 0, 2, 3).reshape(4, 2 * rows_local, width)
    side_a = gathered_direct(sections[:, :, :half], "ty")
    side_b = gathered_direct(sections[:, :, half:], "px")
    pieces = gathered_ring(side_a, "px") + gathered_ring(side_b, "ty")
    pieces = pieces + [in_hbm(shifted(p, "pc", 1)) for p in pieces]
    logits = logits_of(place, pieces, blocks)

    columns = first_column + jnp.arange(cols, dtype=jnp.int32)
    target_hit = targets[:, None] == columns[None, :]
    chosen = jnp.sum(jnp.where(target_hit, logits, f32(0.0)), axis=1)
    local_peak = jnp.max(logits, axis=1)
    local_total = jnp.sum(jnp.exp(logits - local_peak[:, None]), axis=1)
    peak, total, target_logit = joined_all(
        jnp.stack([local_peak, local_total, chosen]), (("pz", "pc", "tz"), ("px", "ty"))
    )
    log_total = peak + jnp.log(total)
    token_loss = lax.dynamic_slice_in_dim(
        log_total - target_logit, (pc * 8 + px * 2 + pz) * rows_local, rows_local, 0
    )

    keep, send = grad_parts(place, logits, log_total, targets, scale, blocks)
    both = [(k + shifted(s, "pc", 1).astype(f32)).astype(bf16) for k, s in zip(keep, send)]
    both = jnp.concatenate(both, axis=1).reshape(32, 4, rows_local, width)
    left = jnp.sum(exchanged(both, NEAR).astype(f32), axis=0)
    return (token_loss, reduced_direct(left, "tz"))


def solution(mesh):
    split = Mesh(mesh.devices.reshape(4, 2, 2, 4, 4), AXES)
    placed = (P(PIPE, TENSOR), P(None, PIPE + TENSOR), P(), P())
    return jax.shard_map(
        local, mesh=split, in_specs=placed, out_specs=(P(PIPE), P(PIPE, TENSOR)), check_vma=False
    )
```
